32 devices in a mesh: dp: 4 (over y, x), tensor: 8 (over z, core).
Axes of the slice: x: 2, y: 2, z: 4, core: 2. Of those that a mesh axis runs over, the one named last changes fastest.
Arguments:
- hidden_acts: bfloat16 [3, 1792, 14336], P(None, 'dp', 'tensor'), may hold values from -6 to 6
- out_grads: bfloat16 [3, 1792, 4096], P(None, 'dp', 'tensor'), may hold values from -6 to 6
Outputs:
- fisher: float32 [14336, 4096], P('tensor', 'dp')
The draws below stay inside these ranges and needn't reach their ends.
All inputs are finite; a program needn't handle non-finite values.
Results may differ from the reference program's by a relative error of at most 0.018.
Values may be sent and summed in bfloat16 or wider, within the bound.
A program may use at most 128 MiB of HBM per device.

```python
import math
import jax
import jax.numpy as jnp
import numpy as np
from jax import lax

D = 4096
FF = 14336
FACTOR_A = 28
SEQS = 3
TOK_DEV = 448
SEQ_LEN = 1792
N_DP = 4


def level_of(own_key, dims, pieces, smallest, high):
    level = 1.0
    for axis_at, parts in pieces:
        draws = jax.random.uniform(jax.random.fold_in(jax.random.fold_in(own_key, 6), axis_at), (parts,), jnp.float32, smallest / len(pieces), high / len(pieces))
        level = level * jnp.repeat(jnp.exp(draws), dims[axis_at] // parts).reshape((-1,) + (1,) * (len(dims) - 1 - axis_at))
    return level


def gaussian(stream_key, shape, deviation, reach, cuts=(), kind=jnp.bfloat16):
    drawn = deviation * jax.random.normal(stream_key, shape, jnp.float32)
    if cuts:
        drawn = drawn * level_of(stream_key, shape, cuts, -0.22, 0.18)
    return jnp.clip(drawn, -reach, reach).astype(kind)


def setup_inputs(seed: int = 0) -> dict:
    arg_keys = jax.random.split(jax.random.key(seed), 3)
    return {
        "hidden_acts": gaussian(arg_keys[0], (SEQS, SEQ_LEN, FF), 1.0, 6.0, ((1, 4), (2, 8))),
        "out_grads": gaussian(arg_keys[1], (SEQS, SEQ_LEN, D), 1.0, 6.0, ((1, 4), (2, 8))),
    }


def sylvester(order):
    result = np.ones((1, 1))
    for doubling in range(order.bit_length() - 1):
        result = np.kron(result, np.array([[1.0, 1.0], [1.0, -1.0]]))
    return result

def paley_matrix():
    residues = set((number * number % 13 for number in range(1, 13)))
    core_table = np.zeros((14, 14))
    core_table[0, 1:] = 1.0
    core_table[1:, 0] = 1.0
    for row_index in range(13):
        for col_index in range(13):
            offset = (col_index - row_index) % 13
            if offset != 0:
                core_table[1 + row_index, 1 + col_index] = 1.0 if offset in residues else -1.0
    return np.kron(core_table, np.array([[1.0, 1.0], [1.0, -1.0]])) + np.kron(np.eye(14), np.array([[1.0, -1.0], [-1.0, -1.0]]))

def reference(hidden_acts, out_grads):
    factor_b = FF // FACTOR_A
    sylvester_table = jnp.asarray(sylvester(factor_b), jnp.float32)
    paley_table = jnp.asarray(paley_matrix(), jnp.float32)
    scaling = 1.0 / math.sqrt(FF)
    inv_root = 1.0 / math.sqrt(SEQ_LEN)
    highest = lax.Precision.HIGHEST
    fisher = jnp.zeros((FF, D), jnp.float32)
    for seq_index in range(SEQS):
        values = hidden_acts[seq_index].astype(jnp.float32).reshape(SEQ_LEN, factor_b, FACTOR_A)
        values = jnp.einsum('lba,bc->lca', values, sylvester_table, precision=highest)
        values = jnp.einsum('lca,ad->lcd', values, paley_table, precision=highest)
        rotated = (values.reshape(SEQ_LEN, FF) * scaling).astype(jnp.bfloat16)
        running = jnp.zeros((FF, D), jnp.float32)
        for block_idx in range(N_DP):
            token_rows = rotated[block_idx * TOK_DEV:(block_idx + 1) * TOK_DEV].astype(jnp.float32)
            grad_rows = out_grads[seq_index, block_idx * TOK_DEV:(block_idx + 1) * TOK_DEV].astype(jnp.float32)
            partial_sum = jnp.dot(token_rows.T, grad_rows, precision=highest)
            rounded = lax.optimization_barrier(partial_sum.astype(jnp.bfloat16))
            running = running + rounded.astype(jnp.float32)
        gradient = running * inv_root
        fisher = fisher + gradient * gradient
    return fisher / SEQS
```

```python
import math

import jax
import jax.numpy as jnp
import numpy as np
from jax import lax
from jax.sharding import PartitionSpec as P

FF = 14336
FACTOR_A = 28
SEQS = 3


def sylvester(order):
    result = np.ones((1, 1))
    for doubling in range(order.bit_length() - 1):
        result = np.kron(result, np.array([[1.0, 1.0], [1.0, -1.0]]))
    return result


def paley_matrix():
    residues = set((number * number % 13 for number in range(1, 13)))
    core_table = np.zeros((14, 14))
    core_table[0, 1:] = 1.0
    core_table[1:, 0] = 1.0
    for row_index in range(13):
        for col_index in range(13):
            offset = (col_index - row_index) % 13
            if offset != 0:
                core_table[1 + row_index, 1 + col_index] = 1.0 if offset in residues else -1.0
    return np.kron(core_table, np.array([[1.0, 1.0], [1.0, -1.0]])) + np.kron(
        np.eye(14), np.array([[1.0, -1.0], [-1.0, -1.0]])
    )


def cross_rotate(values, scaling):
    tok_rows, local_ff = values.shape
    tensor_count = lax.axis_size("tensor")
    mixing = jnp.asarray(sylvester(tensor_count), jnp.float32)
    stacked = values.reshape(tok_rows, 1, local_ff)
    spread = lax.all_to_all(
        stacked.astype(jnp.bfloat16), "tensor", split_axis=0, concat_axis=1, tiled=True
    ).astype(stacked.dtype)
    mixed = jnp.einsum("tqc,qp->tpc", spread, mixing, precision=lax.Precision.HIGHEST)
    scaled = (mixed * scaling).astype(jnp.bfloat16)
    returned = lax.all_to_all(scaled, "tensor", split_axis=1, concat_axis=0, tiled=True)
    return returned.reshape(tok_rows, local_ff)


def on_device(hidden_acts, out_grads):
    seq_count, tok_rows, local_ff = hidden_acts.shape
    dp_count = lax.axis_size("dp")
    local_b = local_ff // FACTOR_A
    local_rot = jnp.asarray(np.kron(sylvester(local_b), paley_matrix()), jnp.bfloat16)
    scaling = 1.0 / math.sqrt(FF)
    inv_root = 1.0 / math.sqrt(tok_rows * dp_count)
    fisher = None
    for seq_index in range(seq_count):
        inner = jnp.dot(hidden_acts[seq_index], local_rot, preferred_element_type=jnp.float32)
        rotated = cross_rotate(inner, scaling)
        grads = lax.all_gather(out_grads[seq_index], "tensor", axis=1, tiled=True)
        grads = lax.all_to_all(grads, "dp", split_axis=1, concat_axis=0, tiled=True)
        gathered = lax.all_gather(rotated, "dp", axis=0, tiled=True)
        summed = lax.dot_general(
            gathered,
            grads,
            (((0,), (0,)), ((), ())),
            preferred_element_type=jnp.float32,
        )
        gradient = summed * inv_root
        fisher = gradient * gradient if fisher is None else fisher + gradient * gradient
    return fisher / SEQS


def solution(mesh):
    placed = (P(None, "dp", "tensor"), P(None, "dp", "tensor"))
    return jax.shard_map(
        on_device, mesh=mesh, in_specs=placed, out_specs=P("tensor", "dp"), check_vma=False
    )
```

```python
import functools
import math

import jax
import jax.numpy as jnp
import numpy as np
from jax import lax
from jax.experimental import pallas as pl
from jax.experimental.pallas import tpu as pltpu
from jax.sharding import PartitionSpec as P

FF = 14336
FACTOR_A = 28
SEQS = 3


def sylvester(order):
    result = np.ones((1, 1))
    for doubling in range(order.bit_length() - 1):
        result = np.kron(result, np.array([[1.0, 1.0], [1.0, -1.0]]))
    return result


def paley_matrix():
    residues = set((number * number % 13 for number in range(1, 13)))
    core_table = np.zeros((14, 14))
    core_table[0, 1:] = 1.0
    core_table[1:, 0] = 1.0
    for row_index in range(13):
        for col_index in range(13):
            offset = (col_index - row_index) % 13
            if offset != 0:
                core_table[1 + row_index, 1 + col_index] = 1.0 if offset in residues else -1.0
    return np.kron(core_table, np.array([[1.0, 1.0], [1.0, -1.0]])) + np.kron(
        np.eye(14), np.array([[1.0, -1.0], [-1.0, -1.0]])
    )


def cross_rotate(values, scaling):
    tok_rows, local_ff = values.shape
    tensor_count = lax.axis_size("tensor")
    mixing = jnp.asarray(sylvester(tensor_count), jnp.float32)
    stacked = values.reshape(tok_rows, 1, local_ff)
    spread = lax.all_to_all(
        stacked.astype(jnp.bfloat16), "tensor", split_axis=0, concat_axis=1, tiled=True
    ).astype(stacked.dtype)
    mixed = jnp.einsum("tqc,qp->tpc", spread, mixing, precision=lax.Precision.HIGHEST)
    scaled = (mixed * scaling).astype(jnp.bfloat16)
    returned = lax.all_to_all(scaled, "tensor", split_axis=1, concat_axis=0, tiled=True)
    return returned.reshape(tok_rows, local_ff)


def on_device(hidden_acts, out_grads):
    seq_count, tok_rows, local_ff = hidden_acts.shape
    dp_count = lax.axis_size("dp")
    local_b = local_ff // FACTOR_A
    local_rot = jnp.asarray(np.kron(sylvester(local_b), paley_matrix()), jnp.bfloat16)
    scaling = 1.0 / math.sqrt(FF)
    inv_root = 1.0 / math.sqrt(tok_rows * dp_count)
    fisher = None
    for seq_index in range(seq_count):
        inner = jnp.dot(hidden_acts[seq_index], local_rot, preferred_element_type=jnp.float32)
        rotated = cross_rotate(inner, scaling)
        grads = lax.all_gather(out_grads[seq_index], "tensor", axis=1, tiled=True)
        grads = lax.all_to_all(grads, "dp", split_axis=1, concat_axis=0, tiled=True)
        gathered = lax.all_gather(rotated, "dp", axis=0, tiled=True)
        summed = lax.dot_general(
            gathered,
            grads,
            (((0,), (0,)), ((), ())),
            preferred_element_type=jnp.float32,
        )
        gradient = summed * inv_root
        fisher = gradient * gradient if fisher is None else fisher + gradient * gradient
    return fisher / SEQS


MESH = pl.DeviceIdType.MESH


def flip(value, mask):
    result = value
    for bit in (1, 2, 4):
        if mask & bit:
            result = result + bit - 2 * bit * ((value // bit) % 2)
    return result


def fisher_kernel(
    sizes, x_ref, g_ref, rot_ref, out_ref, xr, inner, mb, rot, gz, gb,
    send_f, recv_f, send_r, recv_r, send_x, recv_x, send_y, recv_y, send_d, recv_d,
    send_gz, recv_gz, send_gx, recv_gx, send_gp, recv_gp,
):
    seqs, toks, chip_rows, core_rows, scaling, inv_root = sizes
    dpi = lax.axis_index("dp")
    ten = lax.axis_index("tensor")
    z, core = ten // 2, ten % 2
    tensor_count = xr.shape[1]
    chips = tensor_count // 2
    dp_count = rot.shape[1] // toks
    half = rot_ref.shape[0]

    def remote(src, dst, ssem, rsem, dp_to, ten_to):
        return pltpu.make_async_remote_copy(
            src_ref=src, dst_ref=dst, send_sem=ssem, recv_sem=rsem,
            device_id=(dp_to, ten_to), device_id_type=MESH,
        )

    barrier = pltpu.get_barrier_semaphore()
    for d in range(1, tensor_count):
        pl.semaphore_signal(barrier, inc=1, device_id=(dpi, flip(ten, d)), device_id_type=MESH)
    for d in range(1, dp_count):
        pl.semaphore_signal(barrier, inc=1, device_id=(flip(dpi, d), ten), device_id_type=MESH)
    pl.semaphore_wait(barrier, tensor_count + dp_count - 2)

    far_first = [d for pair in range(chips - 1, -1, -1) for d in (2 * pair, 2 * pair + 1)]

    def rows_at(base, count):
        return pl.ds(pl.multiple_of(base, 16), count)

    def spread_copy(s, d, cc):
        to_core = cc ^ (d & 1)
        to = flip(ten, d)
        count = core_rows[to_core]
        base = (to // 2) * chip_rows + to_core * core_rows[0]
        src = x_ref.at[s, rows_at(base, count)]
        dst = xr.at[s, ten, pl.ds(0, count)]
        if d == 0:
            return pltpu.make_async_copy(src, dst, recv_f.at[s, 0])
        return remote(src, dst, send_f.at[s, d], recv_f.at[s, d], dpi, to)

    def start_spread(s):
        for cc in range(2):
            @pl.when(core == cc)
            def _():
                for d in far_first:
                    spread_copy(s, d, cc).start()

    def wait_spread(s):
        for cc in range(2):
            @pl.when(core == cc)
            def _():
                for d in far_first:
                    slot = xr.at[s, flip(ten, d), pl.ds(0, core_rows[cc])]
                    pltpu.make_async_copy(slot, slot, recv_f.at[s, d]).wait()

    def mix(s):
        for h in range(2):
            cols = pl.ds(h * half, half)
            block = xr[s, :, :, cols].reshape(tensor_count * core_rows[0], half)
            inner[:, :, cols] = jnp.dot(
                block, rot_ref[...], preferred_element_type=jnp.float32
            ).reshape(tensor_count, core_rows[0], half)

        def step(i, carry):
            rows = rows_at((i % (core_rows[0] // 16)) * 16, 16)
            lane = (i // (core_rows[0] // 16)) * 128
            parts = [
                inner[q, rows, pl.ds(pl.multiple_of(h * half + lane, 128), 128)]
                for q in range(tensor_count) for h in range(2)
            ]
            stride = 1
            while stride < len(parts):
                mixed = list(parts)
                for at in range(len(parts)):
                    if at & stride == 0:
                        mixed[at] = parts[at] + parts[at + stride]
                        mixed[at + stride] = parts[at] - parts[at + stride]
                parts = mixed
                stride *= 2
            for q in range(tensor_count):
                for h in range(2):
                    mb[s, q, rows, pl.ds(pl.multiple_of(h * half + lane, 128), 128)] = (
                        parts[2 * q + h] * scaling
                    ).astype(jnp.bfloat16)
            return carry

        lax.fori_loop(0, (core_rows[0] // 16) * (half // 128), step, 0)

    def return_copy(s, d, cc):
        to = flip(ten, d)
        count = core_rows[cc]
        src = mb.at[s, to, pl.ds(0, count)]
        dst = rot.at[s, rows_at(dpi * toks + z * chip_rows + cc * core_rows[0], count)]
        if d == 0:
            return pltpu.make_async_copy(src, dst, recv_r.at[s, 0])
        return remote(src, dst, send_r.at[s, d], recv_r.at[s, d], dpi, to)

    def start_return(s):
        for cc in range(2):
            @pl.when(core == cc)
            def _():
                for d in [1, 0] + far_first[:-2]:
                    return_copy(s, d, cc).start()

    def chip_block(s, owner_dp, dz):
        return rot.at[s, rows_at(owner_dp * toks + flip(z, dz) * chip_rows, chip_rows)]

    def start_forward(s, dz):
        for cc in range(2):
            @pl.when(core == cc)
            def _():
                for d in (2 * dz, 2 * dz + 1):
                    from_core = cc ^ (d & 1)
                    piece = rot.at[s, rows_at(
                        dpi * toks + flip(z, dz) * chip_rows + from_core * core_rows[0],
                        core_rows[from_core],
                    )]
                    pltpu.make_async_copy(piece, piece, recv_r.at[s, d]).wait()
        block = chip_block(s, dpi, dz)
        remote(block, block, send_x.at[s, dz], recv_x.at[s, dz], flip(dpi, 1), ten).start()
        remote(block, block, send_y.at[s, dz], recv_y.at[s, dz], flip(dpi, 2), ten).start()

    def wait_block(s, owner_dp, dz, sem):
        block = chip_block(s, owner_dp, dz)
        pltpu.make_async_copy(block, block, sem.at[s, dz]).wait()

    def start_relay(s, dz):
        if dz % 2 == 0:
            wait_block(s, flip(dpi, 1), dz, recv_x)
            block, to = chip_block(s, flip(dpi, 1), dz), flip(dpi, 2)
        else:
            wait_block(s, flip(dpi, 2), dz, recv_y)
            block, to = chip_block(s, flip(dpi, 2), dz), flip(dpi, 1)
        remote(block, block, send_d.at[s, dz], recv_d.at[s, dz], to, ten).start()

    def wait_rest(s):
        for dz in dz_order:
            if dz % 2 == 0:
                wait_block(s, flip(dpi, 2), dz, recv_y)
            else:
                wait_block(s, flip(dpi, 1), dz, recv_x)
            wait_block(s, flip(dpi, 3), dz, recv_d)

    dz_order = [0] + list(range(chips - 1, 0, -1))

    def gz_copy(dz):
        if dz == 0:
            return pltpu.make_async_copy(g_ref, gz.at[z], recv_gz.at[0])
        return remote(g_ref, gz.at[z], send_gz.at[dz], recv_gz.at[dz], dpi, flip(ten, 2 * dz))

    def grad_rows(which, owner_dp):
        return gb.at[which, :, rows_at(owner_dp * toks, toks)]

    def gx_copy(dk):
        to = flip(dpi, dk)
        if dk == 0:
            return pltpu.make_async_copy(gz.at[dpi], grad_rows(core, dpi), recv_gx.at[0])
        return remote(gz.at[to], grad_rows(core, dpi), send_gx.at[dk], recv_gx.at[dk], to, ten)

    def wait_on(ref, sem):
        pltpu.make_async_copy(ref, ref, sem).wait()

    def accumulate(s):
        tile = 256

        def step(m, carry):
            at = pl.ds(pl.multiple_of(m * tile, tile), tile)
            left = rot[s, :, at]
            for which in range(2):
                width = gb.shape[-1]
                cols = pl.ds(which * width, width)
                gradient = lax.dot_general(
                    left, gb[which, s], (((0,), (0,)), ((), ())),
                    preferred_element_type=jnp.float32,
                ) * inv_root
                if s == 0:
                    out_ref[at, cols] = gradient * gradient
                elif s < seqs - 1:
                    out_ref[at, cols] += gradient * gradient
                else:
                    out_ref[at, cols] = (out_ref[at, cols] + gradient * gradient) / seqs
            return carry

        lax.fori_loop(0, out_ref.shape[0] // tile, step, 0)

    start_spread(0)
    if seqs > 1:
        start_spread(1)
    for s in range(seqs):
        wait_spread(s)
        mix(s)
        start_return(s)
        start_forward(s, 0)
        if s + 2 < seqs:
            start_spread(s + 2)
        if s == seqs - 2 or seqs == 1:
            for dz in range(chips - 1, -1, -1):
                gz_copy(dz).start()
        if s >= 1:
            for dz in dz_order[1:]:
                start_forward(s - 1, dz)
            for dz in dz_order:
                start_relay(s - 1, dz)
    for dz in range(chips):
        wait_on(gz.at[flip(z, dz)], recv_gz.at[dz])
    for dk in range(dp_count - 1, -1, -1):
        gx_copy(dk).start()
    for dk in range(dp_count):
        block = grad_rows(core, flip(dpi, dk))
        wait_on(block, recv_gx.at[dk])
        remote(block, block, send_gp.at[dk], recv_gp.at[dk], dpi, flip(ten, 1)).start()
    last = seqs - 1
    for dk in range(dp_count):
        wait_on(grad_rows(1 - core, flip(dpi, dk)), recv_gp.at[dk])
    for s in range(seqs):
        if s == last:
            for dz in dz_order:
                start_relay(s, dz)
        wait_rest(s)
        if s == max(last - 1, 0):
            for dz in dz_order[1:]:
                start_forward(last, dz)
        accumulate(s)
    for s in range(seqs):
        for cc in range(2):
            @pl.when(core == cc)
            def _():
                for d in far_first:
                    if d:
                        spread_copy(s, d, cc).wait_send()
                        return_copy(s, d, cc).wait_send()
        for dz in range(chips):
            block = chip_block(s, dpi, dz)
            remote(block, block, send_x.at[s, dz], recv_x.at[s, dz], flip(dpi, 1), ten).wait_send()
            remote(block, block, send_y.at[s, dz], recv_y.at[s, dz], flip(dpi, 2), ten).wait_send()
            remote(block, block, send_d.at[s, dz], recv_d.at[s, dz], flip(dpi, 1), ten).wait_send()
    for dz in range(1, chips):
        gz_copy(dz).wait_send()
    for dk in range(dp_count):
        if dk:
            gx_copy(dk).wait_send()
        block = grad_rows(core, flip(dpi, dk))
        remote(block, block, send_gp.at[dk], recv_gp.at[dk], dpi, flip(ten, 1)).wait_send()


def fused(hidden_acts, out_grads):
    seqs, toks, local_ff = hidden_acts.shape
    tensor_count, dp_count = lax.axis_size("tensor"), lax.axis_size("dp")
    chips = tensor_count // 2
    width = out_grads.shape[2]
    chip_rows = toks // chips
    first = -(-chip_rows // 32) * 16
    core_rows = (first, chip_rows - first)
    half = local_ff // 2
    local_rot = jnp.asarray(np.kron(sylvester(half // FACTOR_A), paley_matrix()), jnp.bfloat16)
    sizes = (
        seqs, toks, chip_rows, core_rows, 1.0 / math.sqrt(FF), 1.0 / math.sqrt(toks * dp_count)
    )
    dma = pltpu.SemaphoreType.DMA
    return pl.pallas_call(
        functools.partial(fisher_kernel, sizes),
        out_shape=jax.ShapeDtypeStruct((local_ff, 2 * width), jnp.float32),
        in_specs=[
            pl.BlockSpec(memory_space=pl.ANY),
            pl.BlockSpec(memory_space=pl.ANY),
            pl.BlockSpec(memory_space=pltpu.VMEM),
        ],
        out_specs=pl.BlockSpec(memory_space=pltpu.VMEM),
        scratch_shapes=[
            pltpu.VMEM((seqs, tensor_count, first, local_ff), jnp.bfloat16),
            pltpu.VMEM((tensor_count, first, local_ff), jnp.float32),
            pltpu.VMEM((seqs, tensor_count, first, local_ff), jnp.bfloat16),
            pltpu.VMEM((seqs, toks * dp_count, local_ff), jnp.bfloat16),
            pltpu.VMEM((chips, seqs, toks, width), jnp.bfloat16),
            pltpu.VMEM((2, seqs, toks * dp_count, width), jnp.bfloat16),
        ]
        + [dma((seqs, tensor_count))] * 4
        + [dma((seqs, chips))] * 6
        + [dma((chips,))] * 2
        + [dma((dp_count,))] * 4,
        compiler_params=pltpu.CompilerParams(
            collective_id=0, has_side_effects=True, vmem_limit_bytes=67043328
        ),
    )(hidden_acts, out_grads, local_rot)


def fits_fused(mesh):
    tensor_count, dp_count = mesh.shape["tensor"], mesh.shape["dp"]
    local_ff = FF // tensor_count
    return tensor_count == 8 and dp_count == 4 and local_ff % (256 * FACTOR_A // 4) == 0


def solution(mesh):
    placed = (P(None, "dp", "tensor"), P(None, "dp", "tensor"))
    body = fused if fits_fused(mesh) else on_device
    return jax.shard_map(
        body, mesh=mesh, in_specs=placed, out_specs=P("tensor", "dp"), check_vma=False
    )
```

```python
import functools
import math

import jax
import jax.numpy as jnp
import numpy as np
from jax import lax
from jax.experimental import pallas as pl
from jax.experimental.pallas import tpu as pltpu
from jax.sharding import PartitionSpec as P

FF = 14336
FACTOR_A = 28
SEQS = 3


def sylvester(order):
    result = np.ones((1, 1))
    for doubling in range(order.bit_length() - 1):
        result = np.kron(result, np.array([[1.0, 1.0], [1.0, -1.0]]))
    return result


def paley_matrix():
    residues = set((number * number % 13 for number in range(1, 13)))
    core_table = np.zeros((14, 14))
    core_table[0, 1:] = 1.0
    core_table[1:, 0] = 1.0
    for row_index in range(13):
        for col_index in range(13):
            offset = (col_index - row_index) % 13
            if offset != 0:
                core_table[1 + row_index, 1 + col_index] = 1.0 if offset in residues else -1.0
    return np.kron(core_table, np.array([[1.0, 1.0], [1.0, -1.0]])) + np.kron(
        np.eye(14), np.array([[1.0, -1.0], [-1.0, -1.0]])
    )


def cross_rotate(values, scaling):
    tok_rows, local_ff = values.shape
    tensor_count = lax.axis_size("tensor")
    mixing = jnp.asarray(sylvester(tensor_count), jnp.float32)
    stacked = values.reshape(tok_rows, 1, local_ff)
    spread = lax.all_to_all(
        stacked.astype(jnp.bfloat16), "tensor", split_axis=0, concat_axis=1, tiled=True
    ).astype(stacked.dtype)
    mixed = jnp.einsum("tqc,qp->tpc", spread, mixing, precision=lax.Precision.HIGHEST)
    scaled = (mixed * scaling).astype(jnp.bfloat16)
    returned = lax.all_to_all(scaled, "tensor", split_axis=1, concat_axis=0, tiled=True)
    return returned.reshape(tok_rows, local_ff)


def on_device(hidden_acts, out_grads):
    seq_count, tok_rows, local_ff = hidden_acts.shape
    dp_count = lax.axis_size("dp")
    local_b = local_ff // FACTOR_A
    local_rot = jnp.asarray(np.kron(sylvester(local_b), paley_matrix()), jnp.bfloat16)
    scaling = 1.0 / math.sqrt(FF)
    inv_root = 1.0 / math.sqrt(tok_rows * dp_count)
    fisher = None
    for seq_index in range(seq_count):
        inner = jnp.dot(hidden_acts[seq_index], local_rot, preferred_element_type=jnp.float32)
        rotated = cross_rotate(inner, scaling)
        grads = lax.all_gather(out_grads[seq_index], "tensor", axis=1, tiled=True)
        grads = lax.all_to_all(grads, "dp", split_axis=1, concat_axis=0, tiled=True)
        gathered = lax.all_gather(rotated, "dp", axis=0, tiled=True)
        summed = lax.dot_general(
            gathered,
            grads,
            (((0,), (0,)), ((), ())),
            preferred_element_type=jnp.float32,
        )
        gradient = summed * inv_root
        fisher = gradient * gradient if fisher is None else fisher + gradient * gradient
    return fisher / SEQS


MESH = pl.DeviceIdType.MESH


def flip(value, mask):
    result = value
    for bit in (1, 2, 4):
        if mask & bit:
            result = result + bit - 2 * bit * ((value // bit) % 2)
    return result


def fisher_kernel(
    sizes, x_ref, g_ref, rot_ref, out_ref, xr, inner, mb, rot, gz, gb,
    send_f, recv_f, send_r, recv_r, send_x, recv_x, send_y, recv_y, send_d, recv_d,
    send_gz, recv_gz, send_gx, recv_gx, send_gp, recv_gp,
):
    seqs, toks, chip_rows, core_rows, scaling, inv_root = sizes
    dpi = lax.axis_index("dp")
    ten = lax.axis_index("tensor")
    z, core = ten // 2, ten % 2
    tensor_count = xr.shape[1]
    chips = tensor_count // 2
    dp_count = rot.shape[1] // toks
    half = rot_ref.shape[0]

    def remote(src, dst, ssem, rsem, dp_to, ten_to):
        return pltpu.make_async_remote_copy(
            src_ref=src, dst_ref=dst, send_sem=ssem, recv_sem=rsem,
            device_id=(dp_to, ten_to), device_id_type=MESH,
        )

    barrier = pltpu.get_barrier_semaphore()
    for d in range(1, tensor_count):
        pl.semaphore_signal(barrier, inc=1, device_id=(dpi, flip(ten, d)), device_id_type=MESH)
    for d in range(1, dp_count):
        pl.semaphore_signal(barrier, inc=1, device_id=(flip(dpi, d), ten), device_id_type=MESH)
    pl.semaphore_wait(barrier, tensor_count + dp_count - 2)

    near_first = list(range(2, tensor_count)) + [1, 0]

    def rows_at(base, count):
        return pl.ds(pl.multiple_of(base, 16), count)

    def spread_copy(s, d, cc):
        to_core = cc ^ (d & 1)
        to = flip(ten, d)
        count = core_rows[to_core]
        base = (to // 2) * chip_rows + to_core * core_rows[0]
        src = x_ref.at[s, rows_at(base, count)]
        dst = xr.at[s, ten, pl.ds(0, count)]
        if d == 0:
            return pltpu.make_async_copy(src, dst, recv_f.at[s, 0])
        return remote(src, dst, send_f.at[s, d], recv_f.at[s, d], dpi, to)

    def start_spread(s):
        for cc in range(2):
            @pl.when(core == cc)
            def _():
                for d in near_first:
                    spread_copy(s, d, cc).start()

    def wait_spread(s):
        for cc in range(2):
            @pl.when(core == cc)
            def _():
                for d in near_first:
                    slot = xr.at[s, flip(ten, d), pl.ds(0, core_rows[cc])]
                    pltpu.make_async_copy(slot, slot, recv_f.at[s, d]).wait()

    def mix(s):
        for h in range(2):
            cols = pl.ds(h * half, half)
            block = xr[s, :, :, cols].reshape(tensor_count * core_rows[0], half)
            inner[:, :, cols] = jnp.dot(
                block, rot_ref[...], preferred_element_type=jnp.float32
            ).reshape(tensor_count, core_rows[0], half)

        def step(i, carry):
            rows = rows_at((i % (core_rows[0] // 16)) * 16, 16)
            lane = (i // (core_rows[0] // 16)) * 128
            parts = [
                inner[q, rows, pl.ds(pl.multiple_of(h * half + lane, 128), 128)]
                for q in range(tensor_count) for h in range(2)
            ]
            stride = 1
            while stride < len(parts):
                mixed = list(parts)
                for at in range(len(parts)):
                    if at & stride == 0:
                        mixed[at] = parts[at] + parts[at + stride]
                        mixed[at + stride] = parts[at] - parts[at + stride]
                parts = mixed
                stride *= 2
            for q in range(tensor_count):
                for h in range(2):
                    mb[s, q, rows, pl.ds(pl.multiple_of(h * half + lane, 128), 128)] = (
                        parts[2 * q + h] * scaling
                    ).astype(jnp.bfloat16)
            return carry

        lax.fori_loop(0, (core_rows[0] // 16) * (half // 128), step, 0)

    def return_copy(s, d, cc):
        to = flip(ten, d)
        count = core_rows[cc]
        src = mb.at[s, to, pl.ds(0, count)]
        dst = rot.at[s, rows_at(dpi * toks + z * chip_rows + cc * core_rows[0], count)]
        if d == 0:
            return pltpu.make_async_copy(src, dst, recv_r.at[s, 0])
        return remote(src, dst, send_r.at[s, d], recv_r.at[s, d], dpi, to)

    def start_return(s):
        for cc in range(2):
            @pl.when(core == cc)
            def _():
                for d in [1, 0] + near_first[:-2]:
                    return_copy(s, d, cc).start()

    def chip_block(s, owner_dp, dz):
        return rot.at[s, rows_at(owner_dp * toks + flip(z, dz) * chip_rows, chip_rows)]

    def start_forward(s, dz):
        for cc in range(2):
            @pl.when(core == cc)
            def _():
                for d in (2 * dz, 2 * dz + 1):
                    from_core = cc ^ (d & 1)
                    piece = rot.at[s, rows_at(
                        dpi * toks + flip(z, dz) * chip_rows + from_core * core_rows[0],
                        core_rows[from_core],
                    )]
                    pltpu.make_async_copy(piece, piece, recv_r.at[s, d]).wait()
        block = chip_block(s, dpi, dz)
        remote(block, block, send_x.at[s, dz], recv_x.at[s, dz], flip(dpi, 1), ten).start()
        remote(block, block, send_y.at[s, dz], recv_y.at[s, dz], flip(dpi, 2), ten).start()

    def wait_block(s, owner_dp, dz, sem):
        block = chip_block(s, owner_dp, dz)
        pltpu.make_async_copy(block, block, sem.at[s, dz]).wait()

    def start_relay(s, dz):
        if dz % 2 == 0:
            wait_block(s, flip(dpi, 1), dz, recv_x)
            block, to = chip_block(s, flip(dpi, 1), dz), flip(dpi, 2)
        else:
            wait_block(s, flip(dpi, 2), dz, recv_y)
            block, to = chip_block(s, flip(dpi, 2), dz), flip(dpi, 1)
        remote(block, block, send_d.at[s, dz], recv_d.at[s, dz], to, ten).start()

    def wait_rest(s):
        for dz in dz_order:
            if dz % 2 == 0:
                wait_block(s, flip(dpi, 2), dz, recv_y)
            else:
                wait_block(s, flip(dpi, 1), dz, recv_x)
            wait_block(s, flip(dpi, 3), dz, recv_d)

    dz_order = list(range(chips))

    def gz_copy(s, dz):
        src, dst, sem = g_ref.at[s], gz.at[z, s], recv_gz.at[s, dz]
        if dz == 0:
            return pltpu.make_async_copy(src, dst, sem)
        return remote(src, dst, send_gz.at[s, dz], sem, dpi, flip(ten, 2 * dz))

    def grad_rows(which, s, owner_dp):
        return gb.at[which, s, rows_at(owner_dp * toks, toks)]

    def gx_copy(s, dk):
        to = flip(dpi, dk)
        src, dst, sem = gz.at[to, s], grad_rows(core, s, dpi), recv_gx.at[s, dk]
        if dk == 0:
            return pltpu.make_async_copy(src, dst, sem)
        return remote(src, dst, send_gx.at[s, dk], sem, to, ten)

    def gp_copy(s, dk):
        block = grad_rows(core, s, flip(dpi, dk))
        return remote(block, block, send_gp.at[s, dk], recv_gp.at[s, dk], dpi, flip(ten, 1))

    def start_gz(s):
        for dz in list(range(1, chips)) + [0]:
            gz_copy(s, dz).start()

    def start_gx(s):
        for dz in range(chips):
            wait_on(gz.at[flip(z, dz), s], recv_gz.at[s, dz])
        for dk in range(dp_count - 1, -1, -1):
            gx_copy(s, dk).start()

    def start_gp(s):
        for dk in range(dp_count):
            wait_on(grad_rows(core, s, flip(dpi, dk)), recv_gx.at[s, dk])
            gp_copy(s, dk).start()

    def wait_grads(s):
        for dk in range(dp_count):
            wait_on(grad_rows(1 - core, s, flip(dpi, dk)), recv_gp.at[s, dk])

    def gather(s):
        start_relay(s, 0)
        for dz in range(1, chips):
            start_forward(s, dz)
            if dz > 1:
                start_relay(s, dz - 1)
        start_relay(s, chips - 1)

    def wait_on(ref, sem):
        pltpu.make_async_copy(ref, ref, sem).wait()

    def accumulate(s):
        tile = 256

        def step(m, carry):
            at = pl.ds(pl.multiple_of(m * tile, tile), tile)
            left = rot[s, :, at]
            for which in range(2):
                width = gb.shape[-1]
                cols = pl.ds(which * width, width)
                gradient = lax.dot_general(
                    left, gb[which, s], (((0,), (0,)), ((), ())),
                    preferred_element_type=jnp.float32,
                ) * inv_root
                if s == 0:
                    out_ref[at, cols] = gradient * gradient
                elif s < seqs - 1:
                    out_ref[at, cols] += gradient * gradient
                else:
                    out_ref[at, cols] = (out_ref[at, cols] + gradient * gradient) / seqs
            return carry

        lax.fori_loop(0, out_ref.shape[0] // tile, step, 0)

    def rotate(s):
        wait_spread(s)
        mix(s)
        start_return(s)

    last = seqs - 1
    for s in range(last):
        start_gz(s)
    for s in range(last):
        start_spread(s)
    for s in range(last):
        start_gx(s)
    for s in range(last):
        rotate(s)
        if s == 0:
            start_forward(0, 0)
    start_spread(last)
    start_gz(last)
    for s in range(last):
        start_gp(s)
    for s in range(last):
        if s:
            start_forward(s, 0)
        if s == last - 1:
            for done in range(last - 1):
                wait_grads(done)
                wait_rest(done)
                accumulate(done)
        gather(s)
    rotate(last)
    start_forward(last, 0)
    start_gx(last)
    wait_grads(last - 1)
    wait_rest(last - 1)
    accumulate(last - 1)
    start_gp(last)
    gather(last)
    wait_grads(last)
    wait_rest(last)
    accumulate(last)
    for s in range(seqs):
        for cc in range(2):
            @pl.when(core == cc)
            def _():
                for d in near_first:
                    if d:
                        spread_copy(s, d, cc).wait_send()
                        return_copy(s, d, cc).wait_send()
        for dz in range(chips):
            block = chip_block(s, dpi, dz)
            remote(block, block, send_x.at[s, dz], recv_x.at[s, dz], flip(dpi, 1), ten).wait_send()
            remote(block, block, send_y.at[s, dz], recv_y.at[s, dz], flip(dpi, 2), ten).wait_send()
            remote(block, block, send_d.at[s, dz], recv_d.at[s, dz], flip(dpi, 1), ten).wait_send()
        for dz in range(1, chips):
            gz_copy(s, dz).wait_send()
        for dk in range(dp_count):
            if dk:
                gx_copy(s, dk).wait_send()
            gp_copy(s, dk).wait_send()


def fused(hidden_acts, out_grads):
    seqs, toks, local_ff = hidden_acts.shape
    tensor_count, dp_count = lax.axis_size("tensor"), lax.axis_size("dp")
    chips = tensor_count // 2
    width = out_grads.shape[2]
    chip_rows = toks // chips
    first = -(-chip_rows // 32) * 16
    core_rows = (first, chip_rows - first)
    half = local_ff // 2
    local_rot = jnp.asarray(np.kron(sylvester(half // FACTOR_A), paley_matrix()), jnp.bfloat16)
    sizes = (
        seqs, toks, chip_rows, core_rows, 1.0 / math.sqrt(FF), 1.0 / math.sqrt(toks * dp_count)
    )
    dma = pltpu.SemaphoreType.DMA
    return pl.pallas_call(
        functools.partial(fisher_kernel, sizes),
        out_shape=jax.ShapeDtypeStruct((local_ff, 2 * width), jnp.float32),
        in_specs=[
            pl.BlockSpec(memory_space=pl.ANY),
            pl.BlockSpec(memory_space=pl.ANY),
            pl.BlockSpec(memory_space=pltpu.VMEM),
        ],
        out_specs=pl.BlockSpec(memory_space=pltpu.VMEM),
        scratch_shapes=[
            pltpu.VMEM((seqs, tensor_count, first, local_ff), jnp.bfloat16),
            pltpu.VMEM((tensor_count, first, local_ff), jnp.float32),
            pltpu.VMEM((seqs, tensor_count, first, local_ff), jnp.bfloat16),
            pltpu.VMEM((seqs, toks * dp_count, local_ff), jnp.bfloat16),
            pltpu.VMEM((chips, seqs, toks, width), jnp.bfloat16),
            pltpu.VMEM((2, seqs, toks * dp_count, width), jnp.bfloat16),
        ]
        + [dma((seqs, tensor_count))] * 4
        + [dma((seqs, chips))] * 8
        + [dma((seqs, dp_count))] * 4,
        compiler_params=pltpu.CompilerParams(
            collective_id=0, has_side_effects=True, vmem_limit_bytes=67043328
        ),
    )(hidden_acts, out_grads, local_rot)


def fits_fused(mesh):
    tensor_count, dp_count = mesh.shape["tensor"], mesh.shape["dp"]
    local_ff = FF // tensor_count
    return tensor_count == 8 and dp_count == 4 and local_ff % (256 * FACTOR_A // 4) == 0


def solution(mesh):
    placed = (P(None, "dp", "tensor"), P(None, "dp", "tensor"))
    body = fused if fits_fused(mesh) else on_device
    return jax.shard_map(
        body, mesh=mesh, in_specs=placed, out_specs=P("tensor", "dp"), check_vma=False
    )
```

```python
import functools
import math

import jax
import jax.numpy as jnp
import numpy as np
from jax import lax
from jax.experimental import pallas as pl
from jax.experimental.pallas import tpu as pltpu
from jax.sharding import PartitionSpec as P

FF = 14336
FACTOR_A = 28
SEQS = 3


def sylvester(order):
    result = np.ones((1, 1))
    for doubling in range(order.bit_length() - 1):
        result = np.kron(result, np.array([[1.0, 1.0], [1.0, -1.0]]))
    return result


def paley_matrix():
    residues = set((number * number % 13 for number in range(1, 13)))
    core_table = np.zeros((14, 14))
    core_table[0, 1:] = 1.0
    core_table[1:, 0] = 1.0
    for row_index in range(13):
        for col_index in range(13):
            offset = (col_index - row_index) % 13
            if offset != 0:
                core_table[1 + row_index, 1 + col_index] = 1.0 if offset in residues else -1.0
    return np.kron(core_table, np.array([[1.0, 1.0], [1.0, -1.0]])) + np.kron(
        np.eye(14), np.array([[1.0, -1.0], [-1.0, -1.0]])
    )


def cross_rotate(values, scaling):
    tok_rows, local_ff = values.shape
    tensor_count = lax.axis_size("tensor")
    mixing = jnp.asarray(sylvester(tensor_count), jnp.float32)
    stacked = values.reshape(tok_rows, 1, local_ff)
    spread = lax.all_to_all(
        stacked.astype(jnp.bfloat16), "tensor", split_axis=0, concat_axis=1, tiled=True
    ).astype(stacked.dtype)
    mixed = jnp.einsum("tqc,qp->tpc", spread, mixing, precision=lax.Precision.HIGHEST)
    scaled = (mixed * scaling).astype(jnp.bfloat16)
    returned = lax.all_to_all(scaled, "tensor", split_axis=1, concat_axis=0, tiled=True)
    return returned.reshape(tok_rows, local_ff)


def on_device(hidden_acts, out_grads):
    seq_count, tok_rows, local_ff = hidden_acts.shape
    dp_count = lax.axis_size("dp")
    local_b = local_ff // FACTOR_A
    local_rot = jnp.asarray(np.kron(sylvester(local_b), paley_matrix()), jnp.bfloat16)
    scaling = 1.0 / math.sqrt(FF)
    inv_root = 1.0 / math.sqrt(tok_rows * dp_count)
    fisher = None
    for seq_index in range(seq_count):
        inner = jnp.dot(hidden_acts[seq_index], local_rot, preferred_element_type=jnp.float32)
        rotated = cross_rotate(inner, scaling)
        grads = lax.all_gather(out_grads[seq_index], "tensor", axis=1, tiled=True)
        grads = lax.all_to_all(grads, "dp", split_axis=1, concat_axis=0, tiled=True)
        gathered = lax.all_gather(rotated, "dp", axis=0, tiled=True)
        summed = lax.dot_general(
            gathered,
            grads,
            (((0,), (0,)), ((), ())),
            preferred_element_type=jnp.float32,
        )
        gradient = summed * inv_root
        fisher = gradient * gradient if fisher is None else fisher + gradient * gradient
    return fisher / SEQS


MESH = pl.DeviceIdType.MESH


def flip(value, mask):
    result = value
    for bit in (1, 2, 4):
        if mask & bit:
            result = result + bit - 2 * bit * ((value // bit) % 2)
    return result


def fisher_kernel(
    sizes, x_ref, g_ref, rot_ref, out_ref, xr, inner, mb, rot, gz, gb,
    send_f, recv_f, send_r, recv_r, send_x, recv_x, send_y, recv_y, send_d, recv_d,
    send_gz, recv_gz, send_gd, recv_gd, send_gx, recv_gx, send_gp, recv_gp,
):
    seqs, toks, chip_rows, core_rows, scaling, inv_root = sizes
    dpi = lax.axis_index("dp")
    ten = lax.axis_index("tensor")
    z, core = ten // 2, ten % 2
    tensor_count = xr.shape[1]
    chips = tensor_count // 2
    dp_count = rot.shape[1] // toks
    half = rot_ref.shape[0]

    def remote(src, dst, ssem, rsem, dp_to, ten_to):
        return pltpu.make_async_remote_copy(
            src_ref=src, dst_ref=dst, send_sem=ssem, recv_sem=rsem,
            device_id=(dp_to, ten_to), device_id_type=MESH,
        )

    barrier = pltpu.get_barrier_semaphore()
    for d in range(1, tensor_count):
        pl.semaphore_signal(barrier, inc=1, device_id=(dpi, flip(ten, d)), device_id_type=MESH)
    for d in range(1, dp_count):
        pl.semaphore_signal(barrier, inc=1, device_id=(flip(dpi, d), ten), device_id_type=MESH)
    pl.semaphore_wait(barrier, tensor_count + dp_count - 2)

    near_first = list(range(2, tensor_count)) + [1, 0]

    def rows_at(base, count):
        return pl.ds(pl.multiple_of(base, 16), count)

    def spread_copy(s, d, cc):
        to_core = cc ^ (d & 1)
        to = flip(ten, d)
        count = core_rows[to_core]
        base = (to // 2) * chip_rows + to_core * core_rows[0]
        src = x_ref.at[s, rows_at(base, count)]
        dst = xr.at[s, ten, pl.ds(0, count)]
        if d == 0:
            return pltpu.make_async_copy(src, dst, recv_f.at[s, 0])
        return remote(src, dst, send_f.at[s, d], recv_f.at[s, d], dpi, to)

    def start_spread(s):
        for cc in range(2):
            @pl.when(core == cc)
            def _():
                for d in near_first:
                    spread_copy(s, d, cc).start()

    def wait_spread(s):
        for cc in range(2):
            @pl.when(core == cc)
            def _():
                for d in near_first:
                    slot = xr.at[s, flip(ten, d), pl.ds(0, core_rows[cc])]
                    pltpu.make_async_copy(slot, slot, recv_f.at[s, d]).wait()

    def mix(s):
        for h in range(2):
            cols = pl.ds(h * half, half)
            block = xr[s, :, :, cols].reshape(tensor_count * core_rows[0], half)
            inner[:, :, cols] = jnp.dot(
                block, rot_ref[...], preferred_element_type=jnp.float32
            ).reshape(tensor_count, core_rows[0], half)

        def step(i, carry):
            rows = rows_at((i % (core_rows[0] // 16)) * 16, 16)
            lane = (i // (core_rows[0] // 16)) * 128
            parts = [
                inner[q, rows, pl.ds(pl.multiple_of(h * half + lane, 128), 128)]
                for q in range(tensor_count) for h in range(2)
            ]
            stride = 1
            while stride < len(parts):
                mixed = list(parts)
                for at in range(len(parts)):
                    if at & stride == 0:
                        mixed[at] = parts[at] + parts[at + stride]
                        mixed[at + stride] = parts[at] - parts[at + stride]
                parts = mixed
                stride *= 2
            for q in range(tensor_count):
                for h in range(2):
                    mb[s, q, rows, pl.ds(pl.multiple_of(h * half + lane, 128), 128)] = (
                        parts[2 * q + h] * scaling
                    ).astype(jnp.bfloat16)
            return carry

        lax.fori_loop(0, (core_rows[0] // 16) * (half // 128), step, 0)

    def return_copy(s, d, cc):
        to = flip(ten, d)
        count = core_rows[cc]
        src = mb.at[s, to, pl.ds(0, count)]
        dst = rot.at[s, rows_at(dpi * toks + z * chip_rows + cc * core_rows[0], count)]
        if d == 0:
            return pltpu.make_async_copy(src, dst, recv_r.at[s, 0])
        return remote(src, dst, send_r.at[s, d], recv_r.at[s, d], dpi, to)

    def start_return(s):
        for cc in range(2):
            @pl.when(core == cc)
            def _():
                for d in [1, 0] + near_first[:-2]:
                    return_copy(s, d, cc).start()

    def chip_block(s, owner_dp, dz):
        return rot.at[s, rows_at(owner_dp * toks + flip(z, dz) * chip_rows, chip_rows)]

    def start_forward(s, dz):
        for cc in range(2):
            @pl.when(core == cc)
            def _():
                for d in (2 * dz, 2 * dz + 1):
                    from_core = cc ^ (d & 1)
                    piece = rot.at[s, rows_at(
                        dpi * toks + flip(z, dz) * chip_rows + from_core * core_rows[0],
                        core_rows[from_core],
                    )]
                    pltpu.make_async_copy(piece, piece, recv_r.at[s, d]).wait()
        block = chip_block(s, dpi, dz)
        remote(block, block, send_x.at[s, dz], recv_x.at[s, dz], flip(dpi, 1), ten).start()
        remote(block, block, send_y.at[s, dz], recv_y.at[s, dz], flip(dpi, 2), ten).start()

    def wait_block(s, owner_dp, dz, sem):
        block = chip_block(s, owner_dp, dz)
        pltpu.make_async_copy(block, block, sem.at[s, dz]).wait()

    def start_relay(s, dz):
        if dz % 2 == 0:
            wait_block(s, flip(dpi, 1), dz, recv_x)
            block, to = chip_block(s, flip(dpi, 1), dz), flip(dpi, 2)
        else:
            wait_block(s, flip(dpi, 2), dz, recv_y)
            block, to = chip_block(s, flip(dpi, 2), dz), flip(dpi, 1)
        remote(block, block, send_d.at[s, dz], recv_d.at[s, dz], to, ten).start()

    def wait_rest(s):
        for dz in dz_order:
            if dz % 2 == 0:
                wait_block(s, flip(dpi, 2), dz, recv_y)
            else:
                wait_block(s, flip(dpi, 1), dz, recv_x)
            wait_block(s, flip(dpi, 3), dz, recv_d)

    dz_order = list(range(chips))

    def line_copy(s, hop, up):
        own = z - hop if up else z + hop
        src = g_ref.at[s] if hop == 0 else gz.at[own, s]
        ssem, rsem = (send_gz, recv_gz) if up else (send_gd, recv_gd)
        to = ten + 2 if up else ten - 2
        return remote(src, gz.at[own, s], ssem.at[s, hop], rsem.at[s, hop + 1], dpi, to)

    def line_hop(s, hop, action):
        for up in (True, False):
            has = z >= hop if up else z + hop < chips
            goes_on = z + 1 < chips if up else z >= 1

            if action == "start" and hop > 0:
                @pl.when(has)
                def _():
                    own = z - hop if up else z + hop
                    wait_on(gz.at[own, s], (recv_gz if up else recv_gd).at[s, hop])

            if hop < chips - 1:
                @pl.when(jnp.logical_and(has, goes_on))
                def _():
                    copy = line_copy(s, hop, up)
                    if action == "start":
                        copy.start()
                    else:
                        copy.wait_send()

    def own_grad(s):
        return pltpu.make_async_copy(g_ref.at[s], gz.at[z, s], recv_gz.at[s, 0])

    def grad_rows(which, s, owner_dp):
        return gb.at[which, s, rows_at(owner_dp * toks, toks)]

    def gx_copy(s, dk):
        to = flip(dpi, dk)
        src, dst, sem = gz.at[to, s], grad_rows(core, s, dpi), recv_gx.at[s, dk]
        if dk == 0:
            return pltpu.make_async_copy(src, dst, sem)
        return remote(src, dst, send_gx.at[s, dk], sem, to, ten)

    def gp_copy(s, dk):
        block = grad_rows(core, s, flip(dpi, dk))
        return remote(block, block, send_gp.at[s, dk], recv_gp.at[s, dk], dpi, flip(ten, 1))

    def start_gx(s):
        own_grad(s).wait()
        for dk in range(dp_count - 1, -1, -1):
            gx_copy(s, dk).start()

    def start_gp(s):
        for dk in range(dp_count):
            wait_on(grad_rows(core, s, flip(dpi, dk)), recv_gx.at[s, dk])
            gp_copy(s, dk).start()

    def wait_grads(s):
        for dk in range(dp_count):
            wait_on(grad_rows(1 - core, s, flip(dpi, dk)), recv_gp.at[s, dk])

    def gather(s):
        start_relay(s, 0)
        for dz in range(1, chips):
            start_forward(s, dz)
            if dz > 1:
                start_relay(s, dz - 1)
        start_relay(s, chips - 1)

    def wait_on(ref, sem):
        pltpu.make_async_copy(ref, ref, sem).wait()

    def accumulate(s):
        tile = 256

        def step(m, carry):
            at = pl.ds(pl.multiple_of(m * tile, tile), tile)
            left = rot[s, :, at]
            for which in range(2):
                width = gb.shape[-1]
                cols = pl.ds(which * width, width)
                gradient = lax.dot_general(
                    left, gb[which, s], (((0,), (0,)), ((), ())),
                    preferred_element_type=jnp.float32,
                ) * inv_root
                if s == 0:
                    out_ref[at, cols] = gradient * gradient
                elif s < seqs - 1:
                    out_ref[at, cols] += gradient * gradient
                else:
                    out_ref[at, cols] = (out_ref[at, cols] + gradient * gradient) / seqs
            return carry

        lax.fori_loop(0, out_ref.shape[0] // tile, step, 0)

    def rotate(s):
        wait_spread(s)
        mix(s)
        start_return(s)

    last = seqs - 1
    for s in range(seqs):
        own_grad(s).start()
        line_hop(s, 0, "start")
    for hop in range(1, chips - 1):
        for s in range(seqs):
            line_hop(s, hop, "start")
    for s in range(last):
        start_spread(s)
    for s in range(seqs):
        line_hop(s, chips - 1, "start")
        start_gx(s)
    for s in range(last):
        rotate(s)
        if s == 0:
            start_forward(0, 0)
    start_spread(last)
    for s in range(seqs):
        start_gp(s)
    for s in range(last):
        if s:
            start_forward(s, 0)
        if s == last - 1:
            for done in range(last - 1):
                wait_grads(done)
                wait_rest(done)
                accumulate(done)
        gather(s)
    rotate(last)
    start_forward(last, 0)
    wait_grads(last - 1)
    wait_rest(last - 1)
    accumulate(last - 1)
    gather(last)
    wait_grads(last)
    wait_rest(last)
    accumulate(last)
    for s in range(seqs):
        for cc in range(2):
            @pl.when(core == cc)
            def _():
                for d in near_first:
                    if d:
                        spread_copy(s, d, cc).wait_send()
                        return_copy(s, d, cc).wait_send()
        for dz in range(chips):
            block = chip_block(s, dpi, dz)
            remote(block, block, send_x.at[s, dz], recv_x.at[s, dz], flip(dpi, 1), ten).wait_send()
            remote(block, block, send_y.at[s, dz], recv_y.at[s, dz], flip(dpi, 2), ten).wait_send()
            remote(block, block, send_d.at[s, dz], recv_d.at[s, dz], flip(dpi, 1), ten).wait_send()
        for hop in range(chips - 1):
            line_hop(s, hop, "wait")
        for dk in range(dp_count):
            if dk:
                gx_copy(s, dk).wait_send()
            gp_copy(s, dk).wait_send()


def fused(hidden_acts, out_grads):
    seqs, toks, local_ff = hidden_acts.shape
    tensor_count, dp_count = lax.axis_size("tensor"), lax.axis_size("dp")
    chips = tensor_count // 2
    width = out_grads.shape[2]
    chip_rows = toks // chips
    first = -(-chip_rows // 32) * 16
    core_rows = (first, chip_rows - first)
    half = local_ff // 2
    local_rot = jnp.asarray(np.kron(sylvester(half // FACTOR_A), paley_matrix()), jnp.bfloat16)
    sizes = (
        seqs, toks, chip_rows, core_rows, 1.0 / math.sqrt(FF), 1.0 / math.sqrt(toks * dp_count)
    )
    dma = pltpu.SemaphoreType.DMA
    return pl.pallas_call(
        functools.partial(fisher_kernel, sizes),
        out_shape=jax.ShapeDtypeStruct((local_ff, 2 * width), jnp.float32),
        in_specs=[
            pl.BlockSpec(memory_space=pl.ANY),
            pl.BlockSpec(memory_space=pl.ANY),
            pl.BlockSpec(memory_space=pltpu.VMEM),
        ],
        out_specs=pl.BlockSpec(memory_space=pltpu.VMEM),
        scratch_shapes=[
            pltpu.VMEM((seqs, tensor_count, first, local_ff), jnp.bfloat16),
            pltpu.VMEM((tensor_count, first, local_ff), jnp.float32),
            pltpu.VMEM((seqs, tensor_count, first, local_ff), jnp.bfloat16),
            pltpu.VMEM((seqs, toks * dp_count, local_ff), jnp.bfloat16),
            pltpu.VMEM((chips, seqs, toks, width), jnp.bfloat16),
            pltpu.VMEM((2, seqs, toks * dp_count, width), jnp.bfloat16),
        ]
        + [dma((seqs, tensor_count))] * 4
        + [dma((seqs, chips))] * 10
        + [dma((seqs, dp_count))] * 4,
        compiler_params=pltpu.CompilerParams(
            collective_id=0, has_side_effects=True, vmem_limit_bytes=67043328
        ),
    )(hidden_acts, out_grads, local_rot)


def fits_fused(mesh):
    tensor_count, dp_count = mesh.shape["tensor"], mesh.shape["dp"]
    local_ff = FF // tensor_count
    return tensor_count == 8 and dp_count == 4 and local_ff % (256 * FACTOR_A // 4) == 0


def solution(mesh):
    placed = (P(None, "dp", "tensor"), P(None, "dp", "tensor"))
    body = fused if fits_fused(mesh) else on_device
    return jax.shard_map(
        body, mesh=mesh, in_specs=placed, out_specs=P("tensor", "dp"), check_vma=False
    )
```
